32 devices in a mesh: groups: 2 (over x), neuron: 16 (over z, y, core).
Axes of the slice: x: 2, y: 2, z: 4, core: 2. Of those that a mesh axis runs over, the one named last changes fastest.
Arguments:
- queries: bfloat16 [1024, 8, 128], P(('groups', 'neuron')), parts along dimension 0, may hold values from -18 to 18
- keys: bfloat16 [1024, 1024, 128], P(('groups', 'neuron')), parts along dimension 0, may hold values from -6 to 6
- values: bfloat16 [1024, 1024, 128], P(('groups', 'neuron')), parts along dimension 0, may hold values from -6 to 6
- lengths: int32 [256], P('groups'), parts along dimension 0, may hold values from 256 to 1024
- active_blocks: int32 [32, 32], P('groups'), parts along dimension 0, may hold values from 0 to 111, all different within a row
- residual: bfloat16 [256, 4096], P('groups', 'neuron'), parts along dimension 0, may hold values from -18 to 18
- out_weight: bfloat16 [4096, 4096], P(None, 'neuron'), may hold values from -0.09375 to 0.09375
- norm_gain: bfloat16 [4096], P('neuron'), may hold values from 0.099609375 to 1.8984375
- gate_weight: bfloat16 [4096, 14336], P('neuron'), may hold values from -0.09375 to 0.09375
- up_weight: bfloat16 [4096, 14336], P('neuron'), may hold values from -0.09375 to 0.09375
- down_weight: bfloat16 [14336, 4096], P(None, 'neuron'), may hold values from -0.09375 to 0.09375
Outputs:
- layer_out: bfloat16 [256, 4096], P('groups', 'neuron'), parts along dimension 0
The draws below stay inside these ranges and needn't reach their ends.
There are 2 independent parts, one for each index of `groups`. The reference program is written for one: setup_inputs(seed, part) draws one part's arguments, and reference() takes and returns one part's arrays. A program takes and returns all parts, laid end to end along the dimension named above; an argument that names none is the same for every part. Nothing has to cross between parts.
Inputs may be any that keep to these rules, and one draw needn't show every extreme that they name: `active_blocks`: each row names 32 different blocks; every block is named by some row.
All inputs are finite; a program needn't handle non-finite values.
Results may differ from the reference program's by a relative error of at most 0.0052.
Values may be sent and summed in bfloat16 or wider, within the bound.
A program may use at most 128 MiB of HBM per device.

```python
import jax
import jax.numpy as jnp
from jax import lax

D = 4096
KVH = 4
GQ = 8
HD = 128
BLK = 128
NBLK = 112
ACT = 32
G = 16
ROWS = 128
LEN = 1024
H = 32
FF = 14336


def draw_keys(key, part):
    normal = jnp.clip(jax.random.normal(jax.random.fold_in(key, 11), (KVH * ROWS, LEN, HD), jnp.float32), -6.0, 6.0)
    return normal.astype(jnp.bfloat16)


def draw_queries(key, part):
    picked = jnp.clip(3.0 * jax.random.normal(jax.random.fold_in(key, 13), (KVH * ROWS, GQ, HD), jnp.float32), -18.0, 18.0)
    return picked.astype(jnp.bfloat16)


def draw_residual(key, part):
    columns = jnp.arange(D, dtype=jnp.float32) / D
    rough = jax.random.uniform(jax.random.fold_in(key, 17), (D,), jnp.float32, 0.6, 1.4)
    column_scale = 0.5 * jnp.exp(jnp.log(3.0) * columns) * rough
    base = jnp.clip(jax.random.normal(jax.random.fold_in(key, 19), (ROWS, D), jnp.float32), -4.0, 4.0)
    return jnp.clip(base * column_scale[None, :], -18.0, 18.0).astype(jnp.bfloat16)


def set_ends(entries, stream_key, smallest, top_value):
    extent = entries.shape
    spot = [jax.random.randint(jax.random.fold_in(stream_key, axis), (), 0, extent[axis]) for axis in range(len(extent))]
    entries = entries.at[tuple(spot)].set(smallest)
    longest = extent.index(max(extent))
    spot[longest] = (spot[longest] + 1) % extent[longest]
    return entries.at[tuple(spot)].set(top_value)


def steps_of(key, shape, pieces, low, high):
    level = 1.0
    for position, parts in pieces:
        steps = jax.random.uniform(jax.random.fold_in(jax.random.fold_in(key, 6), position), (parts,), jnp.float32, low / len(pieces), high / len(pieces))
        level = level * jnp.repeat(jnp.exp(steps), shape[position] // parts).reshape((-1,) + (1,) * (len(shape) - 1 - position))
    return level


def different_ones(rng, rows, amount, top, lift):
    ranking = jax.random.permutation(jax.random.fold_in(rng, 1), amount)
    boost = ranking
    for power in range(3):
        boost = boost * boost // amount
    boost = boost * lift // amount
    lots = jax.random.randint(jax.random.fold_in(rng, 2), (rows, amount), 0, 4096) + boost
    fixed_rows = jax.random.permutation(jax.random.fold_in(rng, 3), rows)[jnp.arange(amount) % rows]
    lots = jnp.where(jnp.arange(rows)[:, None] == fixed_rows[None, :], 1 << 14, lots)
    score = lots * amount + jnp.arange(amount)
    return lax.top_k(score.astype(jnp.int32), top)[1].astype(jnp.int32)


def noise(own_key, dims, spread, reach, pieces=(), kind=jnp.bfloat16):
    entries = jax.random.normal(own_key, dims, jnp.float32) * spread
    if len(pieces) > 0:
        entries = steps_of(own_key, dims, pieces, -0.22, 0.18) * entries
    return jnp.clip(entries, min=-reach, max=reach).astype(kind)


def setup_inputs(seed: int = 0, part: int = 0) -> dict:
    key_list = jax.random.split(jax.random.key(seed), 12)
    own_keys = jax.random.split(jax.random.fold_in(key_list[11], part), 12)
    queries = draw_queries(jax.random.fold_in(jax.random.fold_in(key_list[11], part), 71), part)
    keys = draw_keys(jax.random.fold_in(jax.random.fold_in(key_list[11], part), 71), part)
    values = noise(own_keys[2], (KVH * ROWS, LEN, HD), 1.0, 6.0, ((0, 16),))
    lengths = set_ends(jax.random.randint(own_keys[3], (ROWS,), LEN // 4, LEN + 1), jax.random.fold_in(own_keys[3], 1), LEN // 4, LEN).astype(jnp.int32)
    active_blocks = different_ones(own_keys[4], G, NBLK, ACT, 2340)
    residual = draw_residual(jax.random.fold_in(jax.random.fold_in(key_list[11], part), 71), part)
    out_weight = noise(key_list[6], (H * HD, D), (H * HD) ** -0.5, 0.09375, ((1, 16),))
    norm_gain = jnp.clip(1.0 + 0.18 * jax.random.normal(key_list[7], (D,), jnp.float32), 0.099609375, 1.8984375).astype(jnp.bfloat16)
    gate_weight = noise(key_list[8], (D, FF), D ** -0.5, 0.09375, ((0, 16),))
    up_weight = noise(key_list[9], (D, FF), D ** -0.5, 0.09375, ((0, 16),))
    down_weight = noise(key_list[10], (FF, D), (ACT * BLK) ** -0.5, 0.09375, ((1, 16),))
    return {"queries": queries, "keys": keys, "values": values, "lengths": lengths, "active_blocks": active_blocks, "residual": residual, "out_weight": out_weight, "norm_gain": norm_gain, "gate_weight": gate_weight, "up_weight": up_weight, "down_weight": down_weight}


def reference(queries, keys, values, lengths, active_blocks, residual, out_weight, norm_gain, gate_weight, up_weight, down_weight):
    entry_rows = jnp.arange(KVH * ROWS, dtype=jnp.int32) % ROWS
    live_lengths = lengths[entry_rows]
    scores = jnp.einsum('egc,etc->egt', queries.astype(jnp.float32), keys.astype(jnp.float32)) * HD ** (-0.5)
    live_mask = jnp.arange(LEN, dtype=jnp.int32)[None, None, :] < live_lengths[:, None, None]
    scores = jnp.where(live_mask, scores, -1e+30)
    running_max = lax.optimization_barrier(jnp.max(scores, axis=-1, keepdims=True))
    weights = jnp.where(live_mask, jnp.exp(scores - running_max), 0.0)
    probs = (weights / lax.optimization_barrier(jnp.sum(weights, axis=-1, keepdims=True))).astype(jnp.bfloat16)
    attended = jnp.einsum('egt,etc->egc', probs.astype(jnp.float32), values.astype(jnp.float32)).astype(jnp.bfloat16)
    by_head = attended.reshape(KVH, ROWS, GQ * HD)
    out_heads = out_weight.reshape(KVH, GQ * HD, D)
    stream = residual.astype(jnp.float32) + jnp.einsum('hrc,hcd->rd', by_head.astype(jnp.float32), out_heads.astype(jnp.float32))
    square_sums = lax.optimization_barrier(jnp.sum(stream * stream, axis=1))
    normed = (stream * lax.rsqrt(square_sums / D + 1e-05)[:, None] * norm_gain.astype(jnp.float32)).astype(jnp.bfloat16)
    group_rows = ROWS // G

    def one_group(operand):
        rows_in, picked = operand
        columns = (picked[:, None] * BLK + jnp.arange(BLK, dtype=jnp.int32)[None, :]).reshape(-1).astype(jnp.int32)
        gate_part = jnp.dot(rows_in, jnp.take(gate_weight, columns, axis=1), preferred_element_type=jnp.float32)
        up_part = jnp.dot(rows_in, jnp.take(up_weight, columns, axis=1), preferred_element_type=jnp.float32)
        activated = (jnp.maximum(gate_part, 0.0) * up_part).astype(jnp.bfloat16)
        return jnp.dot(activated, jnp.take(down_weight, columns, axis=0), preferred_element_type=jnp.float32)
    down_part = lax.map(one_group, (normed.reshape(G, group_rows, D), active_blocks)).reshape(ROWS, D)
    return (stream + down_part).astype(jnp.bfloat16)
```

```python
import functools

import jax
import jax.numpy as jnp
from jax import lax
from jax.experimental import pallas as pl
from jax.experimental.pallas import tpu as pltpu
from jax.sharding import PartitionSpec as P

AXIS = "neuron"
VMEM_LIMIT = 60 * 1024 * 1024


def fitting(total, most):
    size = most
    while total % size:
        size -= 1
    return size


def attention_kernel(lengths, q_ref, k_ref, v_ref, out_ref, held, few, *, per_step, rows):
    step = pl.program_id(0)
    entries, heads = out_ref.shape[0], q_ref.shape[1]
    width, slots = q_ref.shape[2], k_ref.shape[1]
    scale = width ** (-0.5)
    first = lax.rem(lax.axis_index(AXIS) * entries, rows)
    slot = lax.broadcasted_iota(jnp.int32, (heads, slots), 1)
    for i in range(per_step):
        e = step * per_step + i
        live = slot < lengths[first + e]
        scores = lax.dot_general(
            q_ref[i], k_ref[i], (((1,), (1,)), ((), ())), preferred_element_type=jnp.float32
        )
        scores = jnp.where(live, scores * scale, -1e30)
        top = jnp.max(scores, axis=1, keepdims=True)
        weights = jnp.where(live, jnp.exp(scores - top), 0.0)
        total = jnp.sum(weights, axis=1, keepdims=True)
        probs = (weights * (1.0 / total)).astype(jnp.bfloat16)
        mixed = jnp.dot(probs, v_ref[i], preferred_element_type=jnp.float32)
        for j in range(heads):
            few[i : i + 1, j * width : (j + 1) * width] = mixed[j : j + 1, :]
    held[pl.ds(pl.multiple_of(step * per_step, per_step), per_step), :] = few[...]

    @pl.when(step == pl.num_programs(0) - 1)
    def _():
        out_ref[...] = held[...].astype(out_ref.dtype)


def attention(queries, keys, values, lengths):
    entries, heads, width = queries.shape
    slots = keys.shape[1]
    per_step = fitting(entries, 8)
    return pl.pallas_call(
        functools.partial(attention_kernel, per_step=per_step, rows=lengths.shape[0]),
        out_shape=jax.ShapeDtypeStruct((entries, heads * width), jnp.bfloat16),
        grid_spec=pltpu.PrefetchScalarGridSpec(
            num_scalar_prefetch=1,
            grid=(entries // per_step,),
            in_specs=[
                pl.BlockSpec((per_step, heads, width), lambda s, n: (s, 0, 0)),
                pl.BlockSpec((per_step, slots, width), lambda s, n: (s, 0, 0)),
                pl.BlockSpec((per_step, slots, width), lambda s, n: (s, 0, 0)),
            ],
            out_specs=pl.BlockSpec((entries, heads * width), lambda s, n: (0, 0)),
            scratch_shapes=[
                pltpu.VMEM((entries, heads * width), jnp.float32),
                pltpu.VMEM((per_step, heads * width), jnp.float32),
            ],
        ),
        compiler_params=pltpu.CompilerParams(
            dimension_semantics=("arbitrary",), vmem_limit_bytes=VMEM_LIMIT
        ),
        name="attention",
    )(lengths, queries, keys, values)


def up_kernel(picked, x_ref, gate_ref, up_ref, out_ref, gate_all, up_all):
    step = pl.program_id(0)
    blk = gate_all.shape[2]
    per_step = gate_ref.shape[1] // blk
    groups, active = picked.shape
    group_rows = x_ref.shape[0] // groups
    x = x_ref[...]
    for pair in range(0, per_step, 2):
        n = min(2, per_step - pair)
        cols = slice(pair * blk, (pair + n) * blk)
        for w_ref, dense in ((gate_ref, gate_all), (up_ref, up_all)):
            part = jnp.dot(x, w_ref[:, cols], preferred_element_type=jnp.float32)
            for i in range(n):
                dense[step * per_step + pair + i] = part[:, i * blk : (i + 1) * blk]

    @pl.when(step == pl.num_programs(0) - 1)
    def _():
        @pl.loop(0, groups)
        def _(g):
            row = pl.multiple_of(g * group_rows, group_rows)
            for j in range(active):
                b = picked[g, j]
                both = jnp.concatenate(
                    [gate_all[b, pl.ds(row, group_rows), :], up_all[b, pl.ds(row, group_rows), :]],
                    axis=0,
                )
                out_ref[g * active + j] = both.astype(out_ref.dtype)


def project_up(normed, gate_weight, up_weight, picked, blk, out_type):
    rows, width = normed.shape
    ff = gate_weight.shape[1]
    blocks = ff // blk
    groups, active = picked.shape
    group_rows = rows // groups
    per_step = fitting(blocks, 16)
    return pl.pallas_call(
        up_kernel,
        out_shape=jax.ShapeDtypeStruct((groups * active, 2 * group_rows, blk), out_type),
        grid_spec=pltpu.PrefetchScalarGridSpec(
            num_scalar_prefetch=1,
            grid=(blocks // per_step,),
            in_specs=[
                pl.BlockSpec((rows, width), lambda s, n: (0, 0)),
                pl.BlockSpec((width, per_step * blk), lambda s, n: (0, s)),
                pl.BlockSpec((width, per_step * blk), lambda s, n: (0, s)),
            ],
            out_specs=pl.BlockSpec(
                (groups * active, 2 * group_rows, blk), lambda s, n: (0, 0, 0)
            ),
            scratch_shapes=[pltpu.VMEM((blocks, rows, blk), jnp.float32)] * 2,
        ),
        compiler_params=pltpu.CompilerParams(
            dimension_semantics=("arbitrary",), vmem_limit_bytes=VMEM_LIMIT
        ),
        name="project_up",
    )(picked, normed, gate_weight, up_weight)


def down_kernel(picked, act_ref, down_ref, stream_ref, out_ref, dense, total):
    step = pl.program_id(0)
    blk = dense.shape[2]
    per_step = down_ref.shape[0] // blk
    groups, active = picked.shape
    group_rows = dense.shape[1] // groups

    @pl.when(step == 0)
    def _():
        @pl.loop(0, dense.shape[0])
        def _(b):
            dense[b] = jnp.zeros(dense.shape[1:], jnp.float32)

        @pl.loop(0, groups)
        def _(g):
            row = pl.multiple_of(g * group_rows, group_rows)
            for j in range(0, active, 2):
                both = act_ref[(g * active + j) // 2].astype(jnp.float32)
                dense[picked[g, j], pl.ds(row, group_rows), :] = both[:group_rows]
                dense[picked[g, j + 1], pl.ds(row, group_rows), :] = both[group_rows:]

        total[...] = stream_ref[...]

    acc = total[...]
    for pair in range(0, per_step, 2):
        n = min(2, per_step - pair)
        lhs = jnp.concatenate(
            [dense[step * per_step + pair + i] for i in range(n)], axis=1
        ).astype(jnp.bfloat16)
        acc += jnp.dot(
            lhs, down_ref[pair * blk : (pair + n) * blk, :], preferred_element_type=jnp.float32
        )
    total[...] = acc

    @pl.when(step == pl.num_programs(0) - 1)
    def _():
        out_ref[...] = acc.astype(out_ref.dtype)


def project_down(activated, down_weight, stream, picked, blk):
    rows, width = stream.shape
    blocks = down_weight.shape[0] // blk
    per_step = fitting(blocks, 16)
    return pl.pallas_call(
        down_kernel,
        out_shape=jax.ShapeDtypeStruct((rows, width), jnp.bfloat16),
        grid_spec=pltpu.PrefetchScalarGridSpec(
            num_scalar_prefetch=1,
            grid=(blocks // per_step,),
            in_specs=[
                pl.BlockSpec(activated.shape, lambda s, n: (0, 0, 0)),
                pl.BlockSpec((per_step * blk, width), lambda s, n: (s, 0)),
                pl.BlockSpec((rows, width), lambda s, n: (0, 0)),
            ],
            out_specs=pl.BlockSpec((rows, width), lambda s, n: (0, 0)),
            scratch_shapes=[
                pltpu.VMEM((blocks, rows, blk), jnp.float32),
                pltpu.VMEM((rows, width), jnp.float32),
            ],
        ),
        compiler_params=pltpu.CompilerParams(
            dimension_semantics=("arbitrary",), vmem_limit_bytes=VMEM_LIMIT
        ),
        name="project_down",
    )(picked, activated, down_weight, stream)


BLK = 128


def body(
    queries,
    keys,
    values,
    lengths,
    active_blocks,
    residual,
    out_weight,
    norm_gain,
    gate_weight,
    up_weight,
    down_weight,
):
    rows = residual.shape[0]
    groups, active = active_blocks.shape
    group_rows = rows // groups
    members = lax.axis_size(AXIS)
    model = residual.shape[1] * members
    attended = attention(queries, keys, values, lengths)
    gathered = lax.all_gather(attended, AXIS, axis=0, tiled=True)
    by_head = gathered.reshape(gathered.shape[0] // rows, rows, gathered.shape[1])
    out_heads = out_weight.reshape(by_head.shape[0], by_head.shape[2], out_weight.shape[1])
    stream = residual.astype(jnp.float32) + jnp.einsum(
        "hrc,hcd->rd", by_head, out_heads, preferred_element_type=jnp.float32
    )
    square_sums = lax.psum(jnp.sum(stream * stream, axis=1), AXIS)
    normed = (
        stream * lax.rsqrt(square_sums / model + 1e-05)[:, None] * norm_gain.astype(jnp.float32)
    ).astype(jnp.bfloat16)
    parts = project_up(normed, gate_weight, up_weight, active_blocks, BLK, jnp.float32)
    mine = lax.psum_scatter(parts, AXIS, scatter_dimension=0, tiled=True)
    act = (jnp.maximum(mine[:, :group_rows], 0.0) * mine[:, group_rows:]).astype(jnp.bfloat16)
    act = act.reshape(act.shape[0] // 2, 2 * group_rows, act.shape[2])
    activated = lax.all_gather(act, AXIS, axis=0, tiled=True)
    return project_down(activated, down_weight, stream, active_blocks, BLK)


def solution(mesh):
    in_specs = (
        P(("groups", "neuron"), None, None),
        P(("groups", "neuron"), None, None),
        P(("groups", "neuron"), None, None),
        P("groups"),
        P("groups", None),
        P("groups", "neuron"),
        P(None, "neuron"),
        P("neuron"),
        P("neuron", None),
        P("neuron", None),
        P(None, "neuron"),
    )
    out_specs = P("groups", "neuron")
    return jax.shard_map(body, mesh=mesh, in_specs=in_specs, out_specs=out_specs, check_vma=False)
```

```python
import functools

import jax
import jax.numpy as jnp
from jax import lax
from jax.experimental import pallas as pl
from jax.experimental.pallas import tpu as pltpu
from jax.sharding import PartitionSpec as P

AXIS = "neuron"
VMEM_LIMIT = 60 * 1024 * 1024


def fitting(total, most):
    size = most
    while total % size:
        size -= 1
    return size


def attention_kernel(lengths, q_ref, k_ref, v_ref, out_ref, held, few, *, per_step, rows):
    step = pl.program_id(0)
    entries, heads = out_ref.shape[0], q_ref.shape[1]
    width, slots = q_ref.shape[2], k_ref.shape[1]
    scale = width ** (-0.5)
    first = lax.rem(lax.axis_index(AXIS) * entries, rows)
    slot = lax.broadcasted_iota(jnp.int32, (heads, slots), 1)
    for i in range(per_step):
        e = step * per_step + i
        live = slot < lengths[first + e]
        scores = lax.dot_general(
            q_ref[i], k_ref[i], (((1,), (1,)), ((), ())), preferred_element_type=jnp.float32
        )
        scores = jnp.where(live, scores * scale, -1e30)
        top = jnp.max(scores, axis=1, keepdims=True)
        weights = jnp.where(live, jnp.exp(scores - top), 0.0)
        total = jnp.sum(weights, axis=1, keepdims=True)
        probs = (weights * (1.0 / total)).astype(jnp.bfloat16)
        mixed = jnp.dot(probs, v_ref[i], preferred_element_type=jnp.float32)
        for j in range(heads):
            few[i : i + 1, j * width : (j + 1) * width] = mixed[j : j + 1, :]
    held[pl.ds(pl.multiple_of(step * per_step, per_step), per_step), :] = few[...]

    @pl.when(step == pl.num_programs(0) - 1)
    def _():
        out_ref[...] = held[...].astype(out_ref.dtype)


def attention(queries, keys, values, lengths):
    entries, heads, width = queries.shape
    slots = keys.shape[1]
    per_step = fitting(entries, 8)
    return pl.pallas_call(
        functools.partial(attention_kernel, per_step=per_step, rows=lengths.shape[0]),
        out_shape=jax.ShapeDtypeStruct((entries, heads * width), jnp.bfloat16),
        grid_spec=pltpu.PrefetchScalarGridSpec(
            num_scalar_prefetch=1,
            grid=(entries // per_step,),
            in_specs=[
                pl.BlockSpec((per_step, heads, width), lambda s, n: (s, 0, 0)),
                pl.BlockSpec((per_step, slots, width), lambda s, n: (s, 0, 0)),
                pl.BlockSpec((per_step, slots, width), lambda s, n: (s, 0, 0)),
            ],
            out_specs=pl.BlockSpec((entries, heads * width), lambda s, n: (0, 0)),
            scratch_shapes=[
                pltpu.VMEM((entries, heads * width), jnp.float32),
                pltpu.VMEM((per_step, heads * width), jnp.float32),
            ],
        ),
        compiler_params=pltpu.CompilerParams(
            dimension_semantics=("arbitrary",), vmem_limit_bytes=VMEM_LIMIT
        ),
        name="attention",
    )(lengths, queries, keys, values)


def up_kernel(picked, x_ref, gate_ref, up_ref, out_ref, gate_all, up_all):
    step = pl.program_id(0)
    blk = gate_all.shape[2]
    per_step = gate_ref.shape[1] // blk
    groups, active = picked.shape
    group_rows = x_ref.shape[0] // groups
    x = x_ref[...]
    for pair in range(0, per_step, 2):
        n = min(2, per_step - pair)
        cols = slice(pair * blk, (pair + n) * blk)
        for w_ref, dense in ((gate_ref, gate_all), (up_ref, up_all)):
            part = jnp.dot(x, w_ref[:, cols], preferred_element_type=jnp.float32)
            for i in range(n):
                dense[step * per_step + pair + i] = part[:, i * blk : (i + 1) * blk]

    @pl.when(step == pl.num_programs(0) - 1)
    def _():
        @pl.loop(0, groups)
        def _(g):
            row = pl.multiple_of(g * group_rows, group_rows)
            for j in range(active):
                b = picked[g, j]
                both = jnp.concatenate(
                    [gate_all[b, pl.ds(row, group_rows), :], up_all[b, pl.ds(row, group_rows), :]],
                    axis=0,
                )
                out_ref[g * active + j] = both.astype(out_ref.dtype)


def project_up(normed, gate_weight, up_weight, picked, blk, out_type):
    rows, width = normed.shape
    ff = gate_weight.shape[1]
    blocks = ff // blk
    groups, active = picked.shape
    group_rows = rows // groups
    per_step = fitting(blocks, 16)
    return pl.pallas_call(
        up_kernel,
        out_shape=jax.ShapeDtypeStruct((groups * active, 2 * group_rows, blk), out_type),
        grid_spec=pltpu.PrefetchScalarGridSpec(
            num_scalar_prefetch=1,
            grid=(blocks // per_step,),
            in_specs=[
                pl.BlockSpec((rows, width), lambda s, n: (0, 0)),
                pl.BlockSpec((width, per_step * blk), lambda s, n: (0, s)),
                pl.BlockSpec((width, per_step * blk), lambda s, n: (0, s)),
            ],
            out_specs=pl.BlockSpec(
                (groups * active, 2 * group_rows, blk), lambda s, n: (0, 0, 0)
            ),
            scratch_shapes=[pltpu.VMEM((blocks, rows, blk), jnp.float32)] * 2,
        ),
        compiler_params=pltpu.CompilerParams(
            dimension_semantics=("arbitrary",), vmem_limit_bytes=VMEM_LIMIT
        ),
        name="project_up",
    )(picked, normed, gate_weight, up_weight)


def down_kernel(picked, act_ref, down_ref, stream_ref, out_ref, dense, total):
    step = pl.program_id(0)
    blk = dense.shape[2]
    per_step = down_ref.shape[0] // blk
    groups, active = picked.shape
    group_rows = dense.shape[1] // groups

    @pl.when(step == 0)
    def _():
        @pl.loop(0, dense.shape[0])
        def _(b):
            dense[b] = jnp.zeros(dense.shape[1:], jnp.float32)

        @pl.loop(0, groups)
        def _(g):
            row = pl.multiple_of(g * group_rows, group_rows)
            for j in range(0, active, 2):
                both = act_ref[(g * active + j) // 2].astype(jnp.float32)
                dense[picked[g, j], pl.ds(row, group_rows), :] = both[:group_rows]
                dense[picked[g, j + 1], pl.ds(row, group_rows), :] = both[group_rows:]

        total[...] = stream_ref[...]

    acc = total[...]
    for pair in range(0, per_step, 2):
        n = min(2, per_step - pair)
        lhs = jnp.concatenate(
            [dense[step * per_step + pair + i] for i in range(n)], axis=1
        ).astype(jnp.bfloat16)
        acc += jnp.dot(
            lhs, down_ref[pair * blk : (pair + n) * blk, :], preferred_element_type=jnp.float32
        )
    total[...] = acc

    @pl.when(step == pl.num_programs(0) - 1)
    def _():
        out_ref[...] = acc.astype(out_ref.dtype)


def project_down(activated, down_weight, stream, picked, blk):
    rows, width = stream.shape
    blocks = down_weight.shape[0] // blk
    per_step = fitting(blocks, 16)
    return pl.pallas_call(
        down_kernel,
        out_shape=jax.ShapeDtypeStruct((rows, width), jnp.bfloat16),
        grid_spec=pltpu.PrefetchScalarGridSpec(
            num_scalar_prefetch=1,
            grid=(blocks // per_step,),
            in_specs=[
                pl.BlockSpec(activated.shape, lambda s, n: (0, 0, 0)),
                pl.BlockSpec((per_step * blk, width), lambda s, n: (s, 0)),
                pl.BlockSpec((rows, width), lambda s, n: (0, 0)),
            ],
            out_specs=pl.BlockSpec((rows, width), lambda s, n: (0, 0)),
            scratch_shapes=[
                pltpu.VMEM((blocks, rows, blk), jnp.float32),
                pltpu.VMEM((rows, width), jnp.float32),
            ],
        ),
        compiler_params=pltpu.CompilerParams(
            dimension_semantics=("arbitrary",), vmem_limit_bytes=VMEM_LIMIT
        ),
        name="project_down",
    )(picked, activated, down_weight, stream)


MESH = pl.DeviceIdType.MESH


def stage_count(members):
    stages = members.bit_length() - 1
    assert members == 1 << stages
    return stages


def bit_of(me, stage):
    return lax.rem(me // (1 << stage), 2)


def partner_of(me, stage):
    return me + (1 << stage) * (1 - 2 * bit_of(me, stage))


def place_of(me, stages):
    place = 0
    for stage in range(stages):
        place = place + bit_of(me, stage) * (1 << (stages - 1 - stage))
    return place


def static_place(member, stages):
    return sum(((member >> s) & 1) << (stages - 1 - s) for s in range(stages))


def greet(peers):
    barrier = pltpu.get_barrier_semaphore()
    for peer in peers:
        pl.semaphore_signal(barrier, inc=1, device_id={AXIS: peer}, device_id_type=MESH)
    pl.semaphore_wait(barrier, len(peers))


def send(src, dst, send_sem, recv_sem, peer):
    return pltpu.make_async_remote_copy(
        src_ref=src,
        dst_ref=dst,
        send_sem=send_sem,
        recv_sem=recv_sem,
        device_id={AXIS: peer},
        device_id_type=MESH,
    )


def gather_kernel(
    members, rows, att_ref, res_ref, gain_ref, w_hbm, stream_ref, normed_ref,
    held, weight, sums, mine, send_sems, recv_sems, sum_send, sum_recv, own_sem, w_sem,
):
    stages = stage_count(members)
    me = lax.axis_index(AXIS)
    chunks, entries, span = held.shape[0], held.shape[2], held.shape[3]
    w_copy = pltpu.make_async_copy(w_hbm, weight, w_sem)
    w_copy.start()
    place = place_of(me, stages)
    own = [
        pltpu.make_async_copy(
            att_ref.at[:, c * span : (c + 1) * span], held.at[c, place], own_sem.at[c]
        )
        for c in range(chunks)
    ]
    for copy in own:
        copy.start()
    greet([lax.rem(me + step, members) for step in range(1, members)])
    flying = {}

    def start(c, k):
        size = 1 << k
        at = place // size * size
        if k == 0:
            src = att_ref.at[:, c * span : (c + 1) * span]
            dst = held.at[c, place]
        else:
            src = held.at[c, pl.ds(at, size)]
            dst = held.at[c, pl.ds(at, size)]
        copy = send(
            src, dst, send_sems.at[c, k], recv_sems.at[c, k], partner_of(me, stages - 1 - k)
        )
        copy.start()
        flying[c, k] = copy

    for c in range(chunks):
        start(c, 0)
    for copy in own:
        copy.wait()
    for c, k in sorted(
        ((c, k) for c in range(chunks) for k in range(stages)), key=lambda ck: (ck[0] + ck[1], ck[0])
    ):
        flying[c, k].wait_recv()
        if k + 1 < stages:
            start(c, k + 1)
    w_copy.wait()
    total = res_ref[...].astype(jnp.float32)
    per_head = rows // entries
    for head in range(members // per_head):
        for c in range(chunks):
            lhs = jnp.concatenate(
                [held[c, static_place(head * per_head + i, stages)] for i in range(per_head)], axis=0
            )
            first = (head * chunks + c) * span
            total += jnp.dot(
                lhs, weight[first : first + span, :], preferred_element_type=jnp.float32
            )
    stream_ref[...] = total
    lane = sums.shape[2]
    wide = jnp.broadcast_to(jnp.sum(total * total, axis=1, keepdims=True), (rows, lane))
    mine[...] = jnp.transpose(wide)[: mine.shape[0], :]
    copies = []
    for step in range(1, members):
        peer = lax.rem(me + step, members)
        copy = send(mine, sums.at[step], sum_send.at[step], sum_recv.at[step], peer)
        copy.start()
        copies.append(copy)
    row_sums = mine[...]
    for step, copy in enumerate(copies, 1):
        copy.wait_recv()
        row_sums += sums[step]
    spread = jnp.transpose(jnp.broadcast_to(row_sums[:1, :], (lane, rows)))
    model = members * total.shape[1]
    inverse = lax.rsqrt(spread[:, :1] / model + 1e-05)
    normed_ref[...] = (total * inverse * gain_ref[...].astype(jnp.float32)).astype(normed_ref.dtype)
    for copy in copies:
        copy.wait_send()
    for copy in flying.values():
        copy.wait_send()


def gather_and_norm(attended, residual, norm_gain, out_weight, members):
    entries, mixed = attended.shape
    rows, width = residual.shape
    chunks = 2
    stages = stage_count(members)
    vmem = pl.BlockSpec(memory_space=pltpu.VMEM)
    return pl.pallas_call(
        functools.partial(gather_kernel, members, rows),
        out_shape=(
            jax.ShapeDtypeStruct((rows, width), jnp.float32),
            jax.ShapeDtypeStruct((rows, width), jnp.bfloat16),
        ),
        in_specs=[vmem, vmem, vmem, pl.BlockSpec(memory_space=pl.ANY)],
        out_specs=(vmem, vmem),
        scratch_shapes=[
            pltpu.VMEM((chunks, members, entries, mixed // chunks), jnp.bfloat16),
            pltpu.VMEM(out_weight.shape, jnp.bfloat16),
            pltpu.VMEM((members, 8, rows), jnp.float32),
            pltpu.VMEM((8, rows), jnp.float32),
            pltpu.SemaphoreType.DMA((chunks, stages)),
            pltpu.SemaphoreType.DMA((chunks, stages)),
            pltpu.SemaphoreType.DMA((members,)),
            pltpu.SemaphoreType.DMA((members,)),
            pltpu.SemaphoreType.DMA((chunks,)),
            pltpu.SemaphoreType.DMA,
        ],
        compiler_params=pltpu.CompilerParams(
            collective_id=0, has_side_effects=True, vmem_limit_bytes=VMEM_LIMIT
        ),
        name="gather_and_norm",
    )(attended, residual, norm_gain.reshape(1, width), out_weight)


def exchange_kernel(members, chunks, part_ref, act_ref, *scratch):
    stages = stage_count(members)
    me = lax.axis_index(AXIS)
    recv = scratch[:stages]
    out = (None,) + scratch[stages : 2 * stages - 1]
    keep = scratch[2 * stages - 1 : 3 * stages - 2]
    own, held, send_sems, recv_sems = scratch[3 * stages - 2 :]
    size = part_ref.shape[0] // chunks
    group_rows = part_ref.shape[1] // 2
    piece = size // members
    unit = piece // 2
    place = place_of(me, stages)
    greet([partner_of(me, stage) for stage in range(stages)])
    flying = {}

    def go(c, s, src, dst, stage):
        copy = send(src, dst, send_sems.at[c, s], recv_sems.at[c, s], partner_of(me, stage))
        copy.start()
        flying[c, s] = copy

    def start_gather(c, k):
        count = 1 << k
        at = pl.ds((place // count * count) * unit, count * unit)
        src = own.at[c] if k == 0 else held.at[c, at]
        go(c, stages + k, src, held.at[c, at], stages - 1 - k)

    for c in range(chunks):
        half = size // 2
        away = c * size + (1 - bit_of(me, 0)) * half
        go(c, 0, part_ref.at[pl.ds(away, half)], recv[0].at[c], 0)

    def landed(c, s):
        flying[c, s].wait_recv()
        if s >= stages:
            if s + 1 < 2 * stages:
                start_gather(c, s + 1 - stages)
            return
        held_size = size >> (s + 1)

        def added(at, count):
            if s == 0:
                base = c * size + bit_of(me, 0) * held_size
                had = part_ref[pl.ds(base + at, count)].astype(jnp.float32)
            else:
                had = keep[s - 1][c, pl.ds(at, count)]
            return had + recv[s][c, pl.ds(at, count)].astype(jnp.float32)

        if s + 1 < stages:
            half = held_size // 2
            bit = bit_of(me, s + 1)
            out[s + 1][c] = added((1 - bit) * half, half).astype(jnp.bfloat16)
            go(c, s + 1, out[s + 1].at[c], recv[s + 1].at[c], s + 1)
            keep[s][c] = added(bit * half, half)
        else:
            whole = added(0, held_size)
            act = jnp.maximum(whole[:, :group_rows], 0.0) * whole[:, group_rows:]
            act = act.reshape(unit, 2 * group_rows, act.shape[2]).astype(jnp.bfloat16)
            own[c] = act
            start_gather(c, 0)
            held[c, pl.ds(place * unit, unit)] = act

    for c, s in sorted(
        ((c, s) for c in range(chunks) for s in range(2 * stages)),
        key=lambda cs: (cs[1] > 0, cs[0] + cs[1], cs[0]),
    ):
        landed(c, s)
    for c in range(chunks):
        act_ref[pl.ds(c * size // 2, size // 2)] = held[c]
    for copy in flying.values():
        copy.wait_send()


def exchange(parts, members):
    pairs, height, blk = parts.shape
    chunks = 4
    stages = stage_count(members)
    size = pairs // chunks
    vmem = pl.BlockSpec(memory_space=pltpu.VMEM)
    tile = (height, blk)

    def buffers(kind, first, last):
        return [pltpu.VMEM((chunks, size >> (s + 1)) + tile, kind) for s in range(first, last)]

    return pl.pallas_call(
        functools.partial(exchange_kernel, members, chunks),
        out_shape=jax.ShapeDtypeStruct((pairs // 2,) + tile, jnp.bfloat16),
        in_specs=[vmem],
        out_specs=vmem,
        scratch_shapes=buffers(jnp.bfloat16, 0, stages)
        + buffers(jnp.bfloat16, 1, stages)
        + buffers(jnp.float32, 1, stages)
        + [
            pltpu.VMEM((chunks, size // members // 2) + tile, jnp.bfloat16),
            pltpu.VMEM((chunks, size // 2) + tile, jnp.bfloat16),
            pltpu.SemaphoreType.DMA((chunks, 2 * stages)),
            pltpu.SemaphoreType.DMA((chunks, 2 * stages)),
        ],
        compiler_params=pltpu.CompilerParams(
            collective_id=1, has_side_effects=True, vmem_limit_bytes=VMEM_LIMIT
        ),
        name="exchange",
    )(parts)


BLK = 128


def body(
    queries,
    keys,
    values,
    lengths,
    active_blocks,
    residual,
    out_weight,
    norm_gain,
    gate_weight,
    up_weight,
    down_weight,
):
    members = lax.axis_size(AXIS)
    attended = attention(queries, keys, values, lengths)
    stream, normed = gather_and_norm(attended, residual, norm_gain, out_weight, members)
    parts = project_up(normed, gate_weight, up_weight, active_blocks, BLK, jnp.bfloat16)
    activated = exchange(parts, members)
    return project_down(activated, down_weight, stream, active_blocks, BLK)


def solution(mesh):
    in_specs = (
        P(("groups", "neuron"), None, None),
        P(("groups", "neuron"), None, None),
        P(("groups", "neuron"), None, None),
        P("groups"),
        P("groups", None),
        P("groups", "neuron"),
        P(None, "neuron"),
        P("neuron"),
        P("neuron", None),
        P("neuron", None),
        P(None, "neuron"),
    )
    out_specs = P("groups", "neuron")
    return jax.shard_map(body, mesh=mesh, in_specs=in_specs, out_specs=out_specs, check_vma=False)
```

```python
import functools

import jax
import jax.numpy as jnp
from jax import lax
from jax.experimental import pallas as pl
from jax.experimental.pallas import tpu as pltpu
from jax.sharding import PartitionSpec as P

AXIS = "neuron"
VMEM_LIMIT = 60 * 1024 * 1024


def fitting(total, most):
    size = most
    while total % size:
        size -= 1
    return size


def up_kernel(picked, x_ref, gate_ref, up_ref, out_ref, gate_all, up_all):
    step = pl.program_id(0)
    blk = gate_all.shape[2]
    per_step = gate_ref.shape[1] // blk
    groups, active = picked.shape
    group_rows = x_ref.shape[0] // groups
    x = x_ref[...]
    for pair in range(0, per_step, 2):
        n = min(2, per_step - pair)
        cols = slice(pair * blk, (pair + n) * blk)
        for w_ref, dense in ((gate_ref, gate_all), (up_ref, up_all)):
            part = jnp.dot(x, w_ref[:, cols], preferred_element_type=jnp.float32)
            for i in range(n):
                dense[step * per_step + pair + i] = part[:, i * blk : (i + 1) * blk]

    @pl.when(step == pl.num_programs(0) - 1)
    def _():
        @pl.loop(0, groups)
        def _(g):
            row = pl.multiple_of(g * group_rows, group_rows)
            for j in range(active):
                b = picked[g, j]
                both = jnp.concatenate(
                    [gate_all[b, pl.ds(row, group_rows), :], up_all[b, pl.ds(row, group_rows), :]],
                    axis=0,
                )
                out_ref[g * active + j] = both.astype(out_ref.dtype)


def project_up(normed, gate_weight, up_weight, picked, blk, out_type):
    rows, width = normed.shape
    ff = gate_weight.shape[1]
    blocks = ff // blk
    groups, active = picked.shape
    group_rows = rows // groups
    per_step = fitting(blocks, 16)
    return pl.pallas_call(
        up_kernel,
        out_shape=jax.ShapeDtypeStruct((groups * active, 2 * group_rows, blk), out_type),
        grid_spec=pltpu.PrefetchScalarGridSpec(
            num_scalar_prefetch=1,
            grid=(blocks // per_step,),
            in_specs=[
                pl.BlockSpec((rows, width), lambda s, n: (0, 0)),
                pl.BlockSpec((width, per_step * blk), lambda s, n: (0, s)),
                pl.BlockSpec((width, per_step * blk), lambda s, n: (0, s)),
            ],
            out_specs=pl.BlockSpec(
                (groups * active, 2 * group_rows, blk), lambda s, n: (0, 0, 0)
            ),
            scratch_shapes=[pltpu.VMEM((blocks, rows, blk), jnp.float32)] * 2,
        ),
        compiler_params=pltpu.CompilerParams(
            dimension_semantics=("arbitrary",), vmem_limit_bytes=VMEM_LIMIT
        ),
        name="project_up",
    )(picked, normed, gate_weight, up_weight)


def down_kernel(picked, act_ref, stream_ref, down_hbm, out_ref, dense, down, sems):
    blocks, _, blk = dense.shape
    parts = sems.shape[0]
    groups, active = picked.shape
    group_rows = dense.shape[1] // groups
    size = down.shape[0] // parts
    copies = [
        pltpu.make_async_copy(
            down_hbm.at[pl.ds(p * size, size)], down.at[pl.ds(p * size, size)], sems.at[p]
        )
        for p in range(parts)
    ]
    for copy in copies:
        copy.start()

    @pl.loop(0, blocks)
    def _(b):
        dense[b] = jnp.zeros(dense.shape[1:], jnp.float32)

    @pl.loop(0, groups)
    def _(g):
        row = pl.multiple_of(g * group_rows, group_rows)
        for j in range(0, active, 2):
            both = act_ref[(g * active + j) // 2].astype(jnp.float32)
            dense[picked[g, j], pl.ds(row, group_rows), :] = both[:group_rows]
            dense[picked[g, j + 1], pl.ds(row, group_rows), :] = both[group_rows:]

    acc = stream_ref[...]
    per_part = blocks // parts
    for p, copy in enumerate(copies):
        copy.wait()
        for pair in range(p * per_part, (p + 1) * per_part, 2):
            n = min(2, (p + 1) * per_part - pair)
            lhs = jnp.concatenate([dense[pair + i] for i in range(n)], axis=1)
            acc += jnp.dot(
                lhs.astype(jnp.bfloat16),
                down[pair * blk : (pair + n) * blk, :],
                preferred_element_type=jnp.float32,
            )
    out_ref[...] = acc.astype(out_ref.dtype)


def project_down(activated, down_weight, stream, picked, blk):
    rows, width = stream.shape
    blocks = down_weight.shape[0] // blk
    parts = blocks // fitting(blocks, 16)
    vmem = pl.BlockSpec(memory_space=pltpu.VMEM)
    return pl.pallas_call(
        down_kernel,
        out_shape=jax.ShapeDtypeStruct((rows, width), jnp.bfloat16),
        in_specs=[
            pl.BlockSpec(memory_space=pltpu.SMEM),
            vmem,
            vmem,
            pl.BlockSpec(memory_space=pl.ANY),
        ],
        out_specs=vmem,
        scratch_shapes=[
            pltpu.VMEM((blocks, rows, blk), jnp.float32),
            pltpu.VMEM(down_weight.shape, jnp.bfloat16),
            pltpu.SemaphoreType.DMA((parts,)),
        ],
        compiler_params=pltpu.CompilerParams(vmem_limit_bytes=VMEM_LIMIT),
        name="project_down",
    )(picked, activated, stream, down_weight)


MESH = pl.DeviceIdType.MESH


def stage_count(members):
    stages = members.bit_length() - 1
    assert members == 1 << stages
    return stages


def bit_of(me, stage):
    return lax.rem(me // (1 << stage), 2)


def partner_of(me, stage):
    return me + (1 << stage) * (1 - 2 * bit_of(me, stage))


def place_of(me, stages):
    place = 0
    for stage in range(stages):
        place = place + bit_of(me, stage) * (1 << (stages - 1 - stage))
    return place


def static_place(member, stages):
    return sum(((member >> s) & 1) << (stages - 1 - s) for s in range(stages))


def greet(peers):
    barrier = pltpu.get_barrier_semaphore()
    for peer in peers:
        pl.semaphore_signal(barrier, inc=1, device_id={AXIS: peer}, device_id_type=MESH)
    pl.semaphore_wait(barrier, len(peers))


def send(src, dst, send_sem, recv_sem, peer):
    return pltpu.make_async_remote_copy(
        src_ref=src,
        dst_ref=dst,
        send_sem=send_sem,
        recv_sem=recv_sem,
        device_id={AXIS: peer},
        device_id_type=MESH,
    )


def attend(q_ref, keys, values, few, lengths, first, begin):
    heads, width = q_ref.shape[1:]
    count, slots = keys.shape[:2]
    slot = lax.broadcasted_iota(jnp.int32, (heads, slots), 1)
    scores = []
    for i in range(count):
        part = lax.dot_general(
            q_ref[begin + i], keys[i], (((1,), (1,)), ((), ())), preferred_element_type=jnp.float32
        )
        live = slot < lengths[first + begin + i]
        scores.append(jnp.where(live, part * width ** (-0.5), -1e30))
    scores = jnp.concatenate(scores, axis=0)
    weights = jnp.exp(scores - jnp.max(scores, axis=1, keepdims=True))
    probs = weights * (1.0 / jnp.sum(weights, axis=1, keepdims=True))
    probs = probs.astype(jnp.bfloat16)
    for i in range(count):
        mixed = jnp.dot(
            probs[i * heads : (i + 1) * heads], values[i], preferred_element_type=jnp.float32
        )
        for j in range(heads):
            few[i : i + 1, j * width : (j + 1) * width] = mixed[j : j + 1, :]


def gather_kernel(
    members, rows, lengths, q_ref, res_ref, gain_ref, k_hbm, v_hbm, w_hbm, stream_ref, normed_ref,
    keys, values, few, own, held, weight, sums, mine,
    kv_sems, send_sems, recv_sems, sum_send, sum_recv, w_sem,
):
    stages = stage_count(members)
    me = lax.axis_index(AXIS)
    chunks, span = own.shape[0], own.shape[1]
    entries, mixed = chunks * span, own.shape[2]
    place = place_of(me, stages)
    fetched = {}

    def fetch(c):
        for i, (hbm, slots) in enumerate(((k_hbm, keys), (v_hbm, values))):
            copy = pltpu.make_async_copy(
                hbm.at[pl.ds(c * span, span)], slots.at[c % 2], kv_sems.at[i, c % 2]
            )
            copy.start()
            fetched[c, i] = copy

    for c in range(min(2, chunks)):
        fetch(c)
    w_copy = pltpu.make_async_copy(w_hbm, weight, w_sem)
    greet([lax.rem(me + step, members) for step in range(1, members)])
    flying = {}

    def start(c, k):
        size = 1 << k
        at = place // size * size
        src = own.at[c] if k == 0 else held.at[c, pl.ds(at, size)]
        dst = held.at[c, place] if k == 0 else held.at[c, pl.ds(at, size)]
        copy = send(
            src, dst, send_sems.at[c, k], recv_sems.at[c, k], partner_of(me, stages - 1 - k)
        )
        copy.start()
        flying[c, k] = copy

    def landed(c, k):
        flying[c, k].wait_recv()
        if k + 1 < stages:
            start(c, k + 1)

    first = lax.rem(me * entries, rows)
    for c in range(chunks):
        for i in range(2):
            fetched[c, i].wait()
        attend(q_ref, keys.at[c % 2], values.at[c % 2], few, lengths, first, c * span)
        if c + 2 < chunks:
            fetch(c + 2)
        if c == 0:
            w_copy.start()
        block = few[...].astype(jnp.bfloat16)
        own[c] = block
        start(c, 0)
        held[c, place] = block
        for d in range(c):
            if c - d - 1 < stages:
                landed(d, c - d - 1)
    for c, k in sorted(
        ((c, k) for c in range(chunks) for k in range(max(0, chunks - 1 - c), stages)),
        key=lambda ck: (ck[0] + ck[1], ck[0]),
    ):
        landed(c, k)
    w_copy.wait()
    total = res_ref[...].astype(jnp.float32)
    per_head = rows // entries
    for head in range(members // per_head):
        lhs = jnp.concatenate(
            [
                held[c, static_place(head * per_head + i, stages)].astype(jnp.float32)
                for i in range(per_head)
                for c in range(chunks)
            ],
            axis=0,
        ).astype(jnp.bfloat16)
        total += jnp.dot(
            lhs, weight[head * mixed : (head + 1) * mixed, :], preferred_element_type=jnp.float32
        )
    stream_ref[...] = total
    lane = sums.shape[2]
    wide = jnp.broadcast_to(jnp.sum(total * total, axis=1, keepdims=True), (rows, lane))
    mine[...] = jnp.transpose(wide)[: mine.shape[0], :]
    copies = []
    for step in range(1, members):
        peer = lax.rem(me + step, members)
        copy = send(mine, sums.at[step], sum_send.at[step], sum_recv.at[step], peer)
        copy.start()
        copies.append(copy)
    row_sums = mine[...]
    for step, copy in enumerate(copies, 1):
        copy.wait_recv()
        row_sums += sums[step]
    spread = jnp.transpose(jnp.broadcast_to(row_sums[:1, :], (lane, rows)))
    model = members * total.shape[1]
    inverse = lax.rsqrt(spread[:, :1] / model + 1e-05)
    normed_ref[...] = (total * inverse * gain_ref[...].astype(jnp.float32)).astype(normed_ref.dtype)
    for copy in copies:
        copy.wait_send()
    for copy in flying.values():
        copy.wait_send()


def gather_and_norm(queries, keys, values, lengths, residual, norm_gain, out_weight, members):
    entries, heads, head_width = queries.shape
    slots = keys.shape[1]
    rows, width = residual.shape
    span = fitting(entries, 8)
    chunks = entries // span
    mixed = heads * head_width
    stages = stage_count(members)
    vmem = pl.BlockSpec(memory_space=pltpu.VMEM)
    hbm = pl.BlockSpec(memory_space=pl.ANY)
    return pl.pallas_call(
        functools.partial(gather_kernel, members, rows),
        out_shape=(
            jax.ShapeDtypeStruct((rows, width), jnp.float32),
            jax.ShapeDtypeStruct((rows, width), jnp.bfloat16),
        ),
        in_specs=[pl.BlockSpec(memory_space=pltpu.SMEM), vmem, vmem, vmem, hbm, hbm, hbm],
        out_specs=(vmem, vmem),
        scratch_shapes=[
            pltpu.VMEM((2, span, slots, head_width), jnp.bfloat16),
            pltpu.VMEM((2, span, slots, head_width), jnp.bfloat16),
            pltpu.VMEM((span, mixed), jnp.float32),
            pltpu.VMEM((chunks, span, mixed), jnp.bfloat16),
            pltpu.VMEM((chunks, members, span, mixed), jnp.bfloat16),
            pltpu.VMEM(out_weight.shape, jnp.bfloat16),
            pltpu.VMEM((members, 8, rows), jnp.float32),
            pltpu.VMEM((8, rows), jnp.float32),
            pltpu.SemaphoreType.DMA((2, 2)),
            pltpu.SemaphoreType.DMA((chunks, stages)),
            pltpu.SemaphoreType.DMA((chunks, stages)),
            pltpu.SemaphoreType.DMA((members,)),
            pltpu.SemaphoreType.DMA((members,)),
            pltpu.SemaphoreType.DMA,
        ],
        compiler_params=pltpu.CompilerParams(
            collective_id=0, has_side_effects=True, vmem_limit_bytes=VMEM_LIMIT
        ),
        name="gather_and_norm",
    )(lengths, queries, residual, norm_gain.reshape(1, width), keys, values, out_weight)


def exchange_kernel(members, chunks, part_ref, act_ref, *scratch):
    stages = stage_count(members)
    me = lax.axis_index(AXIS)
    recv = scratch[:stages]
    out = (None,) + scratch[stages : 2 * stages - 1]
    keep = scratch[2 * stages - 1 : 3 * stages - 2]
    own, held, send_sems, recv_sems = scratch[3 * stages - 2 :]
    size = part_ref.shape[0] // chunks
    group_rows = part_ref.shape[1] // 2
    piece = size // members
    unit = piece // 2
    place = place_of(me, stages)
    greet([partner_of(me, stage) for stage in range(stages)])
    flying = {}

    def go(c, s, src, dst, stage):
        copy = send(src, dst, send_sems.at[c, s], recv_sems.at[c, s], partner_of(me, stage))
        copy.start()
        flying[c, s] = copy

    def start_gather(c, k):
        count = 1 << k
        at = pl.ds((place // count * count) * unit, count * unit)
        src = own.at[c] if k == 0 else held.at[c, at]
        go(c, stages + k, src, held.at[c, at], stages - 1 - k)

    for c in range(chunks):
        half = size // 2
        away = c * size + (1 - bit_of(me, 0)) * half
        go(c, 0, part_ref.at[pl.ds(away, half)], recv[0].at[c], 0)

    def landed(c, s):
        flying[c, s].wait_recv()
        if s >= stages:
            if s + 1 < 2 * stages:
                start_gather(c, s + 1 - stages)
            return
        held_size = size >> (s + 1)

        def added(at, count):
            if s == 0:
                base = c * size + bit_of(me, 0) * held_size
                had = part_ref[pl.ds(base + at, count)].astype(jnp.float32)
            else:
                had = keep[s - 1][c, pl.ds(at, count)]
            return had + recv[s][c, pl.ds(at, count)].astype(jnp.float32)

        if s + 1 < stages:
            half = held_size // 2
            bit = bit_of(me, s + 1)
            out[s + 1][c] = added((1 - bit) * half, half).astype(jnp.bfloat16)
            go(c, s + 1, out[s + 1].at[c], recv[s + 1].at[c], s + 1)
            keep[s][c] = added(bit * half, half)
        else:
            whole = added(0, held_size)
            act = jnp.maximum(whole[:, :group_rows], 0.0) * whole[:, group_rows:]
            act = act.reshape(unit, 2 * group_rows, act.shape[2]).astype(jnp.bfloat16)
            own[c] = act
            start_gather(c, 0)
            held[c, pl.ds(place * unit, unit)] = act

    for c, s in sorted(
        ((c, s) for c in range(chunks) for s in range(2 * stages)),
        key=lambda cs: (cs[1] > 0, cs[0] + cs[1], cs[0]),
    ):
        landed(c, s)
    for c in range(chunks):
        act_ref[pl.ds(c * size // 2, size // 2)] = held[c]
    for copy in flying.values():
        copy.wait_send()


def exchange(parts, members):
    pairs, height, blk = parts.shape
    chunks = 4
    stages = stage_count(members)
    size = pairs // chunks
    vmem = pl.BlockSpec(memory_space=pltpu.VMEM)
    tile = (height, blk)

    def buffers(kind, first, last):
        return [pltpu.VMEM((chunks, size >> (s + 1)) + tile, kind) for s in range(first, last)]

    return pl.pallas_call(
        functools.partial(exchange_kernel, members, chunks),
        out_shape=jax.ShapeDtypeStruct((pairs // 2,) + tile, jnp.bfloat16),
        in_specs=[vmem],
        out_specs=vmem,
        scratch_shapes=buffers(jnp.bfloat16, 0, stages)
        + buffers(jnp.bfloat16, 1, stages)
        + buffers(jnp.float32, 1, stages)
        + [
            pltpu.VMEM((chunks, size // members // 2) + tile, jnp.bfloat16),
            pltpu.VMEM((chunks, size // 2) + tile, jnp.bfloat16),
            pltpu.SemaphoreType.DMA((chunks, 2 * stages)),
            pltpu.SemaphoreType.DMA((chunks, 2 * stages)),
        ],
        compiler_params=pltpu.CompilerParams(
            collective_id=1, has_side_effects=True, vmem_limit_bytes=VMEM_LIMIT
        ),
        name="exchange",
    )(parts)


BLK = 128


def body(
    queries,
    keys,
    values,
    lengths,
    active_blocks,
    residual,
    out_weight,
    norm_gain,
    gate_weight,
    up_weight,
    down_weight,
):
    members = lax.axis_size(AXIS)
    stream, normed = gather_and_norm(
        queries, keys, values, lengths, residual, norm_gain, out_weight, members
    )
    parts = project_up(normed, gate_weight, up_weight, active_blocks, BLK, jnp.bfloat16)
    activated = exchange(parts, members)
    return project_down(activated, down_weight, stream, active_blocks, BLK)


def solution(mesh):
    in_specs = (
        P(("groups", "neuron"), None, None),
        P(("groups", "neuron"), None, None),
        P(("groups", "neuron"), None, None),
        P("groups"),
        P("groups", None),
        P("groups", "neuron"),
        P(None, "neuron"),
        P("neuron"),
        P("neuron", None),
        P("neuron", None),
        P(None, "neuron"),
    )
    out_specs = P("groups", "neuron")
    return jax.shard_map(body, mesh=mesh, in_specs=in_specs, out_specs=out_specs, check_vma=False)
```

```python
import functools

import jax
import jax.numpy as jnp
from jax import lax
from jax.experimental import pallas as pl
from jax.experimental.pallas import tpu as pltpu
from jax.sharding import PartitionSpec as P

AXIS = "neuron"
VMEM_LIMIT = 60 * 1024 * 1024


def fitting(total, most):
    size = most
    while total % size:
        size -= 1
    return size


def down_kernel(picked, act_ref, stream_ref, down_hbm, out_ref, dense, down, sems):
    blocks, _, blk = dense.shape
    parts = sems.shape[0]
    groups, active = picked.shape
    group_rows = dense.shape[1] // groups
    size = down.shape[0] // parts
    copies = [
        pltpu.make_async_copy(
            down_hbm.at[pl.ds(p * size, size)], down.at[pl.ds(p * size, size)], sems.at[p]
        )
        for p in range(parts)
    ]
    for copy in copies:
        copy.start()

    @pl.loop(0, blocks)
    def _(b):
        dense[b] = jnp.zeros(dense.shape[1:], jnp.float32)

    @pl.loop(0, groups)
    def _(g):
        row = pl.multiple_of(g * group_rows, group_rows)
        for j in range(0, active, 2):
            both = act_ref[(g * active + j) // 2].astype(jnp.float32)
            dense[picked[g, j], pl.ds(row, group_rows), :] = both[:group_rows]
            dense[picked[g, j + 1], pl.ds(row, group_rows), :] = both[group_rows:]

    acc = stream_ref[...]
    per_part = blocks // parts
    for p, copy in enumerate(copies):
        copy.wait()
        for pair in range(p * per_part, (p + 1) * per_part, 2):
            n = min(2, (p + 1) * per_part - pair)
            lhs = jnp.concatenate([dense[pair + i] for i in range(n)], axis=1)
            acc += jnp.dot(
                lhs.astype(jnp.bfloat16),
                down[pair * blk : (pair + n) * blk, :],
                preferred_element_type=jnp.float32,
            )
    out_ref[...] = acc.astype(out_ref.dtype)


def project_down(activated, down_weight, stream, picked, blk):
    rows, width = stream.shape
    blocks = down_weight.shape[0] // blk
    parts = blocks // fitting(blocks, 16)
    vmem = pl.BlockSpec(memory_space=pltpu.VMEM)
    return pl.pallas_call(
        down_kernel,
        out_shape=jax.ShapeDtypeStruct((rows, width), jnp.bfloat16),
        in_specs=[
            pl.BlockSpec(memory_space=pltpu.SMEM),
            vmem,
            vmem,
            pl.BlockSpec(memory_space=pl.ANY),
        ],
        out_specs=vmem,
        scratch_shapes=[
            pltpu.VMEM((blocks, rows, blk), jnp.float32),
            pltpu.VMEM(down_weight.shape, jnp.bfloat16),
            pltpu.SemaphoreType.DMA((parts,)),
        ],
        compiler_params=pltpu.CompilerParams(vmem_limit_bytes=VMEM_LIMIT),
        name="project_down",
    )(picked, activated, stream, down_weight)


MESH = pl.DeviceIdType.MESH


def stage_count(members):
    stages = members.bit_length() - 1
    assert members == 1 << stages
    return stages


def bit_of(me, stage):
    return lax.rem(me // (1 << stage), 2)


def partner_of(me, stage):
    return me + (1 << stage) * (1 - 2 * bit_of(me, stage))


def place_of(me, stages):
    place = 0
    for stage in range(stages):
        place = place + bit_of(me, stage) * (1 << (stages - 1 - stage))
    return place


def static_place(member, stages):
    return sum(((member >> s) & 1) << (stages - 1 - s) for s in range(stages))


def greet(peers):
    barrier = pltpu.get_barrier_semaphore()
    for peer in peers:
        pl.semaphore_signal(barrier, inc=1, device_id={AXIS: peer}, device_id_type=MESH)
    pl.semaphore_wait(barrier, len(peers))


def send(src, dst, send_sem, recv_sem, peer):
    return pltpu.make_async_remote_copy(
        src_ref=src,
        dst_ref=dst,
        send_sem=send_sem,
        recv_sem=recv_sem,
        device_id={AXIS: peer},
        device_id_type=MESH,
    )


def attend(q_ref, keys, values, few, lengths, first, begin):
    heads, width = q_ref.shape[1:]
    count, slots = keys.shape[:2]
    slot = lax.broadcasted_iota(jnp.int32, (heads, slots), 1)
    scores = []
    for i in range(count):
        part = lax.dot_general(
            q_ref[begin + i], keys[i], (((1,), (1,)), ((), ())), preferred_element_type=jnp.float32
        )
        live = slot < lengths[first + begin + i]
        scores.append(jnp.where(live, part * width ** (-0.5), -1e30))
    scores = jnp.concatenate(scores, axis=0)
    weights = jnp.exp(scores - jnp.max(scores, axis=1, keepdims=True))
    probs = weights * (1.0 / jnp.sum(weights, axis=1, keepdims=True))
    probs = probs.astype(jnp.bfloat16)
    for i in range(count):
        mixed = jnp.dot(
            probs[i * heads : (i + 1) * heads], values[i], preferred_element_type=jnp.float32
        )
        for j in range(heads):
            few[i : i + 1, j * width : (j + 1) * width] = mixed[j : j + 1, :]


def layer_kernel(
    members, rows, lengths, picked, q_ref, res_ref, gain_ref, k_hbm, v_hbm, w_hbm, gate_hbm, up_hbm,
    stream_ref, act_ref, keys, values, few, own, held, weight, sums, mine,
    kv_sems, send_sems, recv_sems, sum_send, sum_recv, w_sem,
    gate, up, gate_all, up_all, part_ref, wide_sems, *exchange_scratch,
):
    stages = stage_count(members)
    me = lax.axis_index(AXIS)
    chunks, span = own.shape[0], own.shape[1]
    entries, mixed = chunks * span, own.shape[2]
    place = place_of(me, stages)
    fetched = {}

    def fetch(c):
        for i, (hbm, slots) in enumerate(((k_hbm, keys), (v_hbm, values))):
            copy = pltpu.make_async_copy(
                hbm.at[pl.ds(c * span, span)], slots.at[c % 2], kv_sems.at[i, c % 2]
            )
            copy.start()
            fetched[c, i] = copy

    for c in range(min(2, chunks)):
        fetch(c)
    w_copy = pltpu.make_async_copy(w_hbm, weight, w_sem)
    gate_copy = pltpu.make_async_copy(gate_hbm, gate, wide_sems.at[0])
    up_copy = pltpu.make_async_copy(up_hbm, up, wide_sems.at[1])
    greet([lax.rem(me + step, members) for step in range(1, members)])
    flying = {}

    def start(c, k):
        size = 1 << k
        at = place // size * size
        src = own.at[c] if k == 0 else held.at[c, pl.ds(at, size)]
        dst = held.at[c, place] if k == 0 else held.at[c, pl.ds(at, size)]
        copy = send(
            src, dst, send_sems.at[c, k], recv_sems.at[c, k], partner_of(me, stages - 1 - k)
        )
        copy.start()
        flying[c, k] = copy

    def landed(c, k):
        flying[c, k].wait_recv()
        if k + 1 < stages:
            start(c, k + 1)

    first = lax.rem(me * entries, rows)
    for c in range(chunks):
        for i in range(2):
            fetched[c, i].wait()
        attend(q_ref, keys.at[c % 2], values.at[c % 2], few, lengths, first, c * span)
        if c + 2 < chunks:
            fetch(c + 2)
        if c == 0:
            w_copy.start()
        if c == min(1, chunks - 1):
            gate_copy.start()
            up_copy.start()
        block = few[...].astype(jnp.bfloat16)
        own[c] = block
        start(c, 0)
        held[c, place] = block
        for d in range(c):
            if c - d - 1 < stages:
                landed(d, c - d - 1)
    for c, k in sorted(
        ((c, k) for c in range(chunks) for k in range(max(0, chunks - 1 - c), stages)),
        key=lambda ck: (ck[0] + ck[1], ck[0]),
    ):
        landed(c, k)
    w_copy.wait()
    total = res_ref[...].astype(jnp.float32)
    per_head = rows // entries
    for head in range(members // per_head):
        lhs = jnp.concatenate(
            [
                held[c, static_place(head * per_head + i, stages)].astype(jnp.float32)
                for i in range(per_head)
                for c in range(chunks)
            ],
            axis=0,
        ).astype(jnp.bfloat16)
        total += jnp.dot(
            lhs, weight[head * mixed : (head + 1) * mixed, :], preferred_element_type=jnp.float32
        )
    stream_ref[...] = total
    lane = sums.shape[2]
    wide = jnp.broadcast_to(jnp.sum(total * total, axis=1, keepdims=True), (rows, lane))
    mine[...] = jnp.transpose(wide)[: mine.shape[0], :]
    copies = []
    for step in range(1, members):
        peer = lax.rem(me + step, members)
        copy = send(mine, sums.at[step], sum_send.at[step], sum_recv.at[step], peer)
        copy.start()
        copies.append(copy)
    row_sums = mine[...]
    for step, copy in enumerate(copies, 1):
        copy.wait_recv()
        row_sums += sums[step]
    spread = jnp.transpose(jnp.broadcast_to(row_sums[:1, :], (lane, rows)))
    model = members * total.shape[1]
    inverse = lax.rsqrt(spread[:, :1] / model + 1e-05)
    gain = gain_ref[...].astype(jnp.float32)
    normed = (total * inverse * gain).astype(jnp.bfloat16)
    gate_copy.wait()
    up_copy.wait()
    project_up(normed, gate, up, gate_all, up_all)
    exchange(members, picked, gate_all, up_all, part_ref, act_ref, *exchange_scratch)
    for copy in copies:
        copy.wait_send()
    for copy in flying.values():
        copy.wait_send()


def project_up(normed, gate, up, gate_all, up_all):
    blocks, _, blk = gate_all.shape
    per_dot = fitting(blocks, 2)
    per_step = fitting(blocks // per_dot, 4)
    span = per_dot * blk

    @pl.loop(0, blocks // (per_dot * per_step))
    def _(step):
        for i in range(per_step):
            dot = step * per_step + i
            cols = pl.ds(pl.multiple_of(dot * span, span), span)
            for weight, dense in ((gate, gate_all), (up, up_all)):
                part = jnp.dot(normed, weight[:, cols], preferred_element_type=jnp.float32)
                for n in range(per_dot):
                    dense[dot * per_dot + n] = part[:, n * blk : (n + 1) * blk]


def exchange(members, picked, gate_all, up_all, part_ref, act_ref, *scratch):
    stages = stage_count(members)
    me = lax.axis_index(AXIS)
    recv = scratch[:stages]
    out = (None,) + scratch[stages : 2 * stages - 1]
    keep = scratch[2 * stages - 1 : 3 * stages - 2]
    own, held, send_sems, recv_sems = scratch[3 * stages - 2 :]
    chunks = held.shape[0]
    groups, active = picked.shape
    chunk_groups = groups // chunks
    size = part_ref.shape[0] // chunks
    group_rows = part_ref.shape[1] // 2
    piece = size // members
    unit = piece // 2
    place = place_of(me, stages)
    flying = {}

    def go(c, s, src, dst, stage):
        copy = send(src, dst, send_sems.at[c, s], recv_sems.at[c, s], partner_of(me, stage))
        copy.start()
        flying[c, s] = copy

    def start_gather(c, k):
        count = 1 << k
        at = pl.ds((place // count * count) * unit, count * unit)
        src = own.at[c] if k == 0 else held.at[c, at]
        go(c, stages + k, src, held.at[c, at], stages - 1 - k)

    def pick(c):
        @pl.loop(c * chunk_groups, (c + 1) * chunk_groups)
        def _(g):
            row = pl.multiple_of(g * group_rows, group_rows)
            for j in range(active):
                b = picked[g, j]
                both = jnp.concatenate(
                    [gate_all[b, pl.ds(row, group_rows), :], up_all[b, pl.ds(row, group_rows), :]],
                    axis=0,
                )
                part_ref[g * active + j] = both.astype(part_ref.dtype)

    def start_scatter(c):
        half = size // 2
        away = c * size + (1 - bit_of(me, 0)) * half
        go(c, 0, part_ref.at[pl.ds(away, half)], recv[0].at[c], 0)

    def landed(c, s):
        flying[c, s].wait_recv()
        if s >= stages:
            if s + 1 < 2 * stages:
                start_gather(c, s + 1 - stages)
            return
        held_size = size >> (s + 1)

        def added(at, count):
            if s == 0:
                base = c * size + bit_of(me, 0) * held_size
                had = part_ref[pl.ds(base + at, count)].astype(jnp.float32)
            else:
                had = keep[s - 1][c, pl.ds(at, count)]
            return had + recv[s][c, pl.ds(at, count)].astype(jnp.float32)

        if s + 1 < stages:
            half = held_size // 2
            bit = bit_of(me, s + 1)
            out[s + 1][c] = added((1 - bit) * half, half).astype(jnp.bfloat16)
            go(c, s + 1, out[s + 1].at[c], recv[s + 1].at[c], s + 1)
            keep[s][c] = added(bit * half, half)
        else:
            whole = added(0, held_size)
            act = jnp.maximum(whole[:, :group_rows], 0.0) * whole[:, group_rows:]
            act = act.reshape(unit, 2 * group_rows, act.shape[2]).astype(jnp.bfloat16)
            own[c] = act
            start_gather(c, 0)
            held[c, pl.ds(place * unit, unit)] = act

    for c in range(chunks):
        pick(c)
        start_scatter(c)
    for c, s in sorted(
        ((c, s) for c in range(chunks) for s in range(2 * stages)),
        key=lambda cs: (cs[0] + cs[1], cs[0]),
    ):
        landed(c, s)
    for c in range(chunks):
        act_ref[pl.ds(c * size // 2, size // 2)] = held[c]
    for copy in flying.values():
        copy.wait_send()


def until_activated(
    queries, keys, values, lengths, picked, residual, norm_gain, out_weight, gate_weight, up_weight,
    members, blk,
):
    entries, heads, head_width = queries.shape
    slots = keys.shape[1]
    rows, width = residual.shape
    span = fitting(entries, 8)
    chunks = entries // span
    mixed = heads * head_width
    stages = stage_count(members)
    blocks = gate_weight.shape[1] // blk
    groups, active = picked.shape
    pairs = groups * active
    tile = (2 * rows // groups, blk)
    parts = min(8, groups, pairs // (2 * members))
    size = pairs // parts

    def buffers(kind, begin, end):
        return [pltpu.VMEM((parts, size >> (s + 1)) + tile, kind) for s in range(begin, end)]

    vmem = pl.BlockSpec(memory_space=pltpu.VMEM)
    smem = pl.BlockSpec(memory_space=pltpu.SMEM)
    hbm = pl.BlockSpec(memory_space=pl.ANY)
    return pl.pallas_call(
        functools.partial(layer_kernel, members, rows),
        out_shape=(
            jax.ShapeDtypeStruct((rows, width), jnp.float32),
            jax.ShapeDtypeStruct((pairs // 2,) + tile, jnp.bfloat16),
        ),
        in_specs=[smem, smem, vmem, vmem, vmem, hbm, hbm, hbm, hbm, hbm],
        out_specs=(vmem, vmem),
        scratch_shapes=[
            pltpu.VMEM((2, span, slots, head_width), jnp.bfloat16),
            pltpu.VMEM((2, span, slots, head_width), jnp.bfloat16),
            pltpu.VMEM((span, mixed), jnp.float32),
            pltpu.VMEM((chunks, span, mixed), jnp.bfloat16),
            pltpu.VMEM((chunks, members, span, mixed), jnp.bfloat16),
            pltpu.VMEM(out_weight.shape, jnp.bfloat16),
            pltpu.VMEM((members, 8, rows), jnp.float32),
            pltpu.VMEM((8, rows), jnp.float32),
            pltpu.SemaphoreType.DMA((2, 2)),
            pltpu.SemaphoreType.DMA((chunks, stages)),
            pltpu.SemaphoreType.DMA((chunks, stages)),
            pltpu.SemaphoreType.DMA((members,)),
            pltpu.SemaphoreType.DMA((members,)),
            pltpu.SemaphoreType.DMA,
            pltpu.VMEM(gate_weight.shape, jnp.bfloat16),
            pltpu.VMEM(up_weight.shape, jnp.bfloat16),
            pltpu.VMEM((blocks, rows, blk), jnp.float32),
            pltpu.VMEM((blocks, rows, blk), jnp.float32),
            pltpu.VMEM((pairs,) + tile, jnp.bfloat16),
            pltpu.SemaphoreType.DMA((2,)),
        ]
        + buffers(jnp.bfloat16, 0, stages)
        + buffers(jnp.bfloat16, 1, stages)
        + buffers(jnp.float32, 1, stages)
        + [
            pltpu.VMEM((parts, size // members // 2) + tile, jnp.bfloat16),
            pltpu.VMEM((parts, size // 2) + tile, jnp.bfloat16),
            pltpu.SemaphoreType.DMA((parts, 2 * stages)),
            pltpu.SemaphoreType.DMA((parts, 2 * stages)),
        ],
        compiler_params=pltpu.CompilerParams(
            collective_id=0, has_side_effects=True, vmem_limit_bytes=VMEM_LIMIT
        ),
        name="until_activated",
    )(
        lengths, picked, queries, residual, norm_gain.reshape(1, width),
        keys, values, out_weight, gate_weight, up_weight,
    )


BLK = 128


def body(
    queries,
    keys,
    values,
    lengths,
    active_blocks,
    residual,
    out_weight,
    norm_gain,
    gate_weight,
    up_weight,
    down_weight,
):
    members = lax.axis_size(AXIS)
    stream, activated = until_activated(
        queries, keys, values, lengths, active_blocks, residual, norm_gain, out_weight,
        gate_weight, up_weight, members, BLK,
    )
    return project_down(activated, down_weight, stream, active_blocks, BLK)


def solution(mesh):
    in_specs = (
        P(("groups", "neuron"), None, None),
        P(("groups", "neuron"), None, None),
        P(("groups", "neuron"), None, None),
        P("groups"),
        P("groups", None),
        P("groups", "neuron"),
        P(None, "neuron"),
        P("neuron"),
        P("neuron", None),
        P("neuron", None),
        P(None, "neuron"),
    )
    out_specs = P("groups", "neuron")
    return jax.shard_map(body, mesh=mesh, in_specs=in_specs, out_specs=out_specs, check_vma=False)
```

```python
import functools

import jax
import jax.numpy as jnp
from jax import lax
from jax.experimental import pallas as pl
from jax.experimental.pallas import tpu as pltpu
from jax.sharding import PartitionSpec as P

AXIS = "neuron"
VMEM_LIMIT = 60 * 1024 * 1024


def fitting(total, most):
    size = most
    while total % size:
        size -= 1
    return size


def down_kernel(picked, act_ref, stream_ref, down_hbm, out_ref, dense, down, sems):
    blocks, _, blk = dense.shape
    parts = sems.shape[0]
    groups, active = picked.shape
    group_rows = dense.shape[1] // groups
    size = down.shape[0] // parts
    copies = [
        pltpu.make_async_copy(
            down_hbm.at[pl.ds(p * size, size)], down.at[pl.ds(p * size, size)], sems.at[p]
        )
        for p in range(parts)
    ]
    for copy in copies:
        copy.start()

    @pl.loop(0, blocks)
    def _(b):
        dense[b] = jnp.zeros(dense.shape[1:], jnp.float32)

    @pl.loop(0, groups)
    def _(g):
        row = pl.multiple_of(g * group_rows, group_rows)
        for j in range(0, active, 2):
            both = act_ref[(g * active + j) // 2].astype(jnp.float32)
            dense[picked[g, j], pl.ds(row, group_rows), :] = both[:group_rows]
            dense[picked[g, j + 1], pl.ds(row, group_rows), :] = both[group_rows:]

    acc = stream_ref[...]
    per_part = blocks // parts
    for p, copy in enumerate(copies):
        copy.wait()
        for pair in range(p * per_part, (p + 1) * per_part, 2):
            n = min(2, (p + 1) * per_part - pair)
            lhs = jnp.concatenate([dense[pair + i] for i in range(n)], axis=1)
            acc += jnp.dot(
                lhs.astype(jnp.bfloat16),
                down[pair * blk : (pair + n) * blk, :],
                preferred_element_type=jnp.float32,
            )
    out_ref[...] = acc.astype(out_ref.dtype)


def project_down(activated, down_weight, stream, picked, blk):
    rows, width = stream.shape
    blocks = down_weight.shape[0] // blk
    parts = blocks // fitting(blocks, 16)
    vmem = pl.BlockSpec(memory_space=pltpu.VMEM)
    return pl.pallas_call(
        down_kernel,
        out_shape=jax.ShapeDtypeStruct((rows, width), jnp.bfloat16),
        in_specs=[
            pl.BlockSpec(memory_space=pltpu.SMEM),
            vmem,
            vmem,
            pl.BlockSpec(memory_space=pl.ANY),
        ],
        out_specs=vmem,
        scratch_shapes=[
            pltpu.VMEM((blocks, rows, blk), jnp.float32),
            pltpu.VMEM(down_weight.shape, jnp.bfloat16),
            pltpu.SemaphoreType.DMA((parts,)),
        ],
        compiler_params=pltpu.CompilerParams(vmem_limit_bytes=VMEM_LIMIT),
        name="project_down",
    )(picked, activated, stream, down_weight)


MESH = pl.DeviceIdType.MESH


def stage_count(members):
    stages = members.bit_length() - 1
    assert members == 1 << stages
    return stages


def bit_of(me, stage):
    return lax.rem(me // (1 << stage), 2)


def partner_of(me, stage):
    return me + (1 << stage) * (1 - 2 * bit_of(me, stage))


def place_of(me, stages):
    place = 0
    for stage in range(stages):
        place = place + bit_of(me, stage) * (1 << (stages - 1 - stage))
    return place


def static_place(member, stages):
    return sum(((member >> s) & 1) << (stages - 1 - s) for s in range(stages))


def greet(peers):
    barrier = pltpu.get_barrier_semaphore()
    for peer in peers:
        pl.semaphore_signal(barrier, inc=1, device_id={AXIS: peer}, device_id_type=MESH)
    pl.semaphore_wait(barrier, len(peers))


def send(src, dst, send_sem, recv_sem, peer):
    return pltpu.make_async_remote_copy(
        src_ref=src,
        dst_ref=dst,
        send_sem=send_sem,
        recv_sem=recv_sem,
        device_id={AXIS: peer},
        device_id_type=MESH,
    )


def attend(q_ref, keys, values, few, lengths, first, begin):
    heads, width = q_ref.shape[1:]
    count, slots = keys.shape[:2]
    slot = lax.broadcasted_iota(jnp.int32, (heads, slots), 1)
    scores = []
    for i in range(count):
        part = lax.dot_general(
            q_ref[begin + i], keys[i], (((1,), (1,)), ((), ())), preferred_element_type=jnp.float32
        )
        live = slot < lengths[first + begin + i]
        scores.append(jnp.where(live, part * width ** (-0.5), -1e30))
    scores = jnp.concatenate(scores, axis=0)
    weights = jnp.exp(scores - jnp.max(scores, axis=1, keepdims=True))
    probs = weights * (1.0 / jnp.sum(weights, axis=1, keepdims=True))
    probs = probs.astype(jnp.bfloat16)
    for i in range(count):
        mixed = jnp.dot(
            probs[i * heads : (i + 1) * heads], values[i], preferred_element_type=jnp.float32
        )
        for j in range(heads):
            few[i : i + 1, j * width : (j + 1) * width] = mixed[j : j + 1, :]


def layer_kernel(
    members, rows, lengths, picked, q_ref, res_ref, gain_ref, k_hbm, v_hbm, w_hbm, gate_hbm, up_hbm,
    stream_ref, act_ref, keys, values, few, own, held, weight, sums, mine,
    kv_sems, send_sems, recv_sems, sum_send, sum_recv, w_sem,
    gate, up, gate_all, up_all, part_ref, inverse, wide_sems, *exchange_scratch,
):
    stages = stage_count(members)
    me = lax.axis_index(AXIS)
    chunks, span = own.shape[0], own.shape[1]
    entries, mixed = chunks * span, own.shape[2]
    place = place_of(me, stages)
    fetched = {}

    def fetch(c):
        for i, (hbm, slots) in enumerate(((k_hbm, keys), (v_hbm, values))):
            copy = pltpu.make_async_copy(
                hbm.at[pl.ds(c * span, span)], slots.at[c % 2], kv_sems.at[i, c % 2]
            )
            copy.start()
            fetched[c, i] = copy

    for c in range(min(2, chunks)):
        fetch(c)
    w_copy = pltpu.make_async_copy(w_hbm, weight, w_sem)
    gate_copy = pltpu.make_async_copy(gate_hbm, gate, wide_sems.at[0])
    up_copy = pltpu.make_async_copy(up_hbm, up, wide_sems.at[1])
    greet([lax.rem(me + step, members) for step in range(1, members)])
    flying = {}

    def start(c, k):
        size = 1 << k
        at = place // size * size
        src = own.at[c] if k == 0 else held.at[c, pl.ds(at, size)]
        dst = held.at[c, place] if k == 0 else held.at[c, pl.ds(at, size)]
        copy = send(
            src, dst, send_sems.at[c, k], recv_sems.at[c, k], partner_of(me, stages - 1 - k)
        )
        copy.start()
        flying[c, k] = copy

    def landed(c, k):
        flying[c, k].wait_recv()
        if k + 1 < stages:
            start(c, k + 1)

    first = lax.rem(me * entries, rows)
    for c in range(chunks):
        for i in range(2):
            fetched[c, i].wait()
        attend(q_ref, keys.at[c % 2], values.at[c % 2], few, lengths, first, c * span)
        if c + 2 < chunks:
            fetch(c + 2)
        if c == 0:
            w_copy.start()
        if c == min(1, chunks - 1):
            gate_copy.start()
            up_copy.start()
        block = few[...].astype(jnp.bfloat16)
        own[c] = block
        start(c, 0)
        held[c, place] = block
        for d in range(c):
            if c - d - 1 < stages:
                landed(d, c - d - 1)
    for c, k in sorted(
        ((c, k) for c in range(chunks) for k in range(max(0, chunks - 1 - c), stages)),
        key=lambda ck: (ck[0] + ck[1], ck[0]),
    ):
        landed(c, k)
    w_copy.wait()
    total = res_ref[...].astype(jnp.float32)
    per_head = rows // entries
    for head in range(members // per_head):
        lhs = jnp.concatenate(
            [
                held[c, static_place(head * per_head + i, stages)].astype(jnp.float32)
                for i in range(per_head)
                for c in range(chunks)
            ],
            axis=0,
        ).astype(jnp.bfloat16)
        total += jnp.dot(
            lhs, weight[head * mixed : (head + 1) * mixed, :], preferred_element_type=jnp.float32
        )
    stream_ref[...] = total
    lane = sums.shape[2]
    wide = jnp.broadcast_to(jnp.sum(total * total, axis=1, keepdims=True), (rows, lane))
    mine[...] = jnp.transpose(wide)[: mine.shape[0], :]
    copies = []
    for step in range(1, members):
        peer = lax.rem(me + step, members)
        copy = send(mine, sums.at[step], sum_send.at[step], sum_recv.at[step], peer)
        copy.start()
        copies.append(copy)
    scaled = (total * gain_ref[...].reshape(1, total.shape[1]).astype(jnp.float32)).astype(jnp.bfloat16)
    gate_copy.wait()
    up_copy.wait()
    project_up(scaled, gate, up, gate_all, up_all)
    row_sums = mine[...]
    for step, copy in enumerate(copies, 1):
        copy.wait_recv()
        row_sums += sums[step]
    spread = jnp.transpose(jnp.broadcast_to(row_sums[:1, :], (inverse.shape[1], rows)))
    model = members * total.shape[1]
    inverse[...] = lax.rsqrt(spread / model + 1e-05)
    exchange(members, picked, inverse, gate_all, up_all, part_ref, act_ref, *exchange_scratch)
    for copy in copies:
        copy.wait_send()
    for copy in flying.values():
        copy.wait_send()


def project_up(normed, gate, up, gate_all, up_all):
    blocks, _, blk = gate_all.shape
    per_dot = fitting(blocks, 2)
    per_step = fitting(blocks // per_dot, 4)
    span = per_dot * blk

    @pl.loop(0, blocks // (per_dot * per_step))
    def _(step):
        for i in range(per_step):
            dot = step * per_step + i
            cols = pl.ds(pl.multiple_of(dot * span, span), span)
            for weight, dense in ((gate, gate_all), (up, up_all)):
                part = jnp.dot(normed, weight[:, cols], preferred_element_type=jnp.float32)
                for n in range(per_dot):
                    dense[dot * per_dot + n] = part[:, n * blk : (n + 1) * blk]


def exchange(members, picked, inverse, gate_all, up_all, part_ref, act_ref, *scratch):
    stages = stage_count(members)
    me = lax.axis_index(AXIS)
    recv = scratch[:stages]
    out = (None,) + scratch[stages : 2 * stages - 1]
    keep = scratch[2 * stages - 1 : 3 * stages - 2]
    own, held, send_sems, recv_sems = scratch[3 * stages - 2 :]
    chunks = held.shape[0]
    groups, active = picked.shape
    chunk_groups = groups // chunks
    size = part_ref.shape[0] // chunks
    group_rows = part_ref.shape[1] // 2
    piece = size // members
    unit = piece // 2
    place = place_of(me, stages)
    flying = {}

    def go(c, s, src, dst, stage):
        copy = send(src, dst, send_sems.at[c, s], recv_sems.at[c, s], partner_of(me, stage))
        copy.start()
        flying[c, s] = copy

    def start_gather(c, k):
        count = 1 << k
        at = pl.ds((place // count * count) * unit, count * unit)
        src = own.at[c] if k == 0 else held.at[c, at]
        go(c, stages + k, src, held.at[c, at], stages - 1 - k)

    def pick(c):
        @pl.loop(c * chunk_groups, (c + 1) * chunk_groups)
        def _(g):
            row = pl.multiple_of(g * group_rows, group_rows)
            scale = inverse[pl.ds(row, group_rows), :]
            for j in range(active):
                b = picked[g, j]
                both = jnp.concatenate(
                    [
                        gate_all[b, pl.ds(row, group_rows), :] * scale,
                        up_all[b, pl.ds(row, group_rows), :] * scale,
                    ],
                    axis=0,
                )
                part_ref[g * active + j] = both.astype(part_ref.dtype)

    def start_scatter(c):
        half = size // 2
        away = c * size + (1 - bit_of(me, 0)) * half
        go(c, 0, part_ref.at[pl.ds(away, half)], recv[0].at[c], 0)

    def landed(c, s):
        flying[c, s].wait_recv()
        if s >= stages:
            if s + 1 < 2 * stages:
                start_gather(c, s + 1 - stages)
            return
        held_size = size >> (s + 1)

        def added(at, count):
            if s == 0:
                base = c * size + bit_of(me, 0) * held_size
                had = part_ref[pl.ds(base + at, count)].astype(jnp.float32)
            else:
                had = keep[s - 1][c, pl.ds(at, count)]
            return had + recv[s][c, pl.ds(at, count)].astype(jnp.float32)

        if s + 1 < stages:
            half = held_size // 2
            bit = bit_of(me, s + 1)
            out[s + 1][c] = added((1 - bit) * half, half).astype(jnp.bfloat16)
            go(c, s + 1, out[s + 1].at[c], recv[s + 1].at[c], s + 1)
            keep[s][c] = added(bit * half, half)
        else:
            whole = added(0, held_size)
            act = jnp.maximum(whole[:, :group_rows], 0.0) * whole[:, group_rows:]
            act = act.reshape(unit, 2 * group_rows, act.shape[2]).astype(jnp.bfloat16)
            own[c] = act
            start_gather(c, 0)
            held[c, pl.ds(place * unit, unit)] = act

    for c in range(chunks):
        pick(c)
        start_scatter(c)
    for c, s in sorted(
        ((c, s) for c in range(chunks) for s in range(2 * stages)),
        key=lambda cs: (cs[0] + cs[1], cs[0]),
    ):
        landed(c, s)
    for c in range(chunks):
        act_ref[pl.ds(c * size // 2, size // 2)] = held[c]
    for copy in flying.values():
        copy.wait_send()


def until_activated(
    queries, keys, values, lengths, picked, residual, norm_gain, out_weight, gate_weight, up_weight,
    members, blk,
):
    entries, heads, head_width = queries.shape
    slots = keys.shape[1]
    rows, width = residual.shape
    span = fitting(entries, 8)
    chunks = entries // span
    mixed = heads * head_width
    stages = stage_count(members)
    blocks = gate_weight.shape[1] // blk
    groups, active = picked.shape
    pairs = groups * active
    tile = (2 * rows // groups, blk)
    parts = min(8, groups, pairs // (2 * members))
    size = pairs // parts

    def buffers(kind, begin, end):
        return [pltpu.VMEM((parts, size >> (s + 1)) + tile, kind) for s in range(begin, end)]

    vmem = pl.BlockSpec(memory_space=pltpu.VMEM)
    smem = pl.BlockSpec(memory_space=pltpu.SMEM)
    hbm = pl.BlockSpec(memory_space=pl.ANY)
    return pl.pallas_call(
        functools.partial(layer_kernel, members, rows),
        out_shape=(
            jax.ShapeDtypeStruct((rows, width), jnp.float32),
            jax.ShapeDtypeStruct((pairs // 2,) + tile, jnp.bfloat16),
        ),
        in_specs=[smem, smem, vmem, vmem, vmem, hbm, hbm, hbm, hbm, hbm],
        out_specs=(vmem, vmem),
        scratch_shapes=[
            pltpu.VMEM((2, span, slots, head_width), jnp.bfloat16),
            pltpu.VMEM((2, span, slots, head_width), jnp.bfloat16),
            pltpu.VMEM((span, mixed), jnp.float32),
            pltpu.VMEM((chunks, span, mixed), jnp.bfloat16),
            pltpu.VMEM((chunks, members, span, mixed), jnp.bfloat16),
            pltpu.VMEM(out_weight.shape, jnp.bfloat16),
            pltpu.VMEM((members, 8, rows), jnp.float32),
            pltpu.VMEM((8, rows), jnp.float32),
            pltpu.SemaphoreType.DMA((2, 2)),
            pltpu.SemaphoreType.DMA((chunks, stages)),
            pltpu.SemaphoreType.DMA((chunks, stages)),
            pltpu.SemaphoreType.DMA((members,)),
            pltpu.SemaphoreType.DMA((members,)),
            pltpu.SemaphoreType.DMA,
            pltpu.VMEM(gate_weight.shape, jnp.bfloat16),
            pltpu.VMEM(up_weight.shape, jnp.bfloat16),
            pltpu.VMEM((blocks, rows, blk), jnp.float32),
            pltpu.VMEM((blocks, rows, blk), jnp.float32),
            pltpu.VMEM((pairs,) + tile, jnp.bfloat16),
            pltpu.VMEM((rows, blk), jnp.float32),
            pltpu.SemaphoreType.DMA((2,)),
        ]
        + buffers(jnp.bfloat16, 0, stages)
        + buffers(jnp.bfloat16, 1, stages)
        + buffers(jnp.float32, 1, stages)
        + [
            pltpu.VMEM((parts, size // members // 2) + tile, jnp.bfloat16),
            pltpu.VMEM((parts, size // 2) + tile, jnp.bfloat16),
            pltpu.SemaphoreType.DMA((parts, 2 * stages)),
            pltpu.SemaphoreType.DMA((parts, 2 * stages)),
        ],
        compiler_params=pltpu.CompilerParams(
            collective_id=0, has_side_effects=True, vmem_limit_bytes=VMEM_LIMIT
        ),
        name="until_activated",
    )(
        lengths, picked, queries, residual, norm_gain,
        keys, values, out_weight, gate_weight, up_weight,
    )


BLK = 128


def body(
    queries,
    keys,
    values,
    lengths,
    active_blocks,
    residual,
    out_weight,
    norm_gain,
    gate_weight,
    up_weight,
    down_weight,
):
    members = lax.axis_size(AXIS)
    stream, activated = until_activated(
        queries, keys, values, lengths, active_blocks, residual, norm_gain, out_weight,
        gate_weight, up_weight, members, BLK,
    )
    return project_down(activated, down_weight, stream, active_blocks, BLK)


def solution(mesh):
    in_specs = (
        P(("groups", "neuron"), None, None),
        P(("groups", "neuron"), None, None),
        P(("groups", "neuron"), None, None),
        P("groups"),
        P("groups", None),
        P("groups", "neuron"),
        P(None, "neuron"),
        P("neuron"),
        P("neuron", None),
        P("neuron", None),
        P(None, "neuron"),
    )
    out_specs = P("groups", "neuron")
    return jax.shard_map(body, mesh=mesh, in_specs=in_specs, out_specs=out_specs, check_vma=False)
```
